128 devices in a mesh: seq: 4 (over z), exp: 32 (over y, x, core).
Axes of the slice: x: 4, y: 4, z: 4, core: 2. Of those that a mesh axis runs over, the one named last changes fastest.
Arguments:
- attn_inputs: bfloat16 [32, 512, 6144], P('exp', 'seq'), may hold values from -8 to 8
- residual: bfloat16 [32, 512, 2048], P('exp', 'seq'), may hold values from -6 to 6
- out_weight: bfloat16 [2048, 2048], P('exp'), may hold values from -0.125 to 0.125
- norm_gain: float32 [2048], replicated, may hold values from 0.1 to 1.9
- expert_ids: int32 [32, 512, 2], P('exp', 'seq'), may hold values from 0 to 31, all different within a row; in each aligned block of 128 rows (0 to 127, 128 to 255, ..., all dimensions but the last counted through in order) at most 10 rows name the same one
- gate_weights: float32 [32, 512, 2], P('exp', 'seq'), may hold values from 0.1 to 1
- gate_weight: bfloat16 [32, 2048, 5632], P('exp', None, 'seq'), may hold values from -0.125 to 0.125
- up_weight: bfloat16 [32, 2048, 5632], P('exp', None, 'seq'), may hold values from -0.125 to 0.125
- down_weight: bfloat16 [32, 5632, 2048], P('exp', 'seq'), may hold values from -0.078125 to 0.078125
Outputs:
- layer_out: bfloat16 [32, 512, 2048], P('exp', 'seq')
The draws below stay inside these ranges and needn't reach their ends.
Inputs may be any that keep to these rules, and one draw needn't show every extreme that they name: `expert_ids`: each token names 2 different experts; in every draw no expert is named by more than 10 of the 128 tokens of one aligned block of rows (the rows of one device), and some block reaches 10.
All inputs are finite; a program needn't handle non-finite values.
Results may differ from the reference program's by a relative error of at most 0.013.
Values may be sent and summed in bfloat16 or wider, within the bound.
A program may use at most 128 MiB of HBM per device.

```python
import math
import jax
import jax.numpy as jnp
import numpy as np
from jax import lax

D = 2048
HEADS = 16
HEAD_DIM = 128
FF = 5632
TOP = 2
TOK_DEV = 128
EXPERTS = 32
CAP = 10
CLIPS = 32
CLIP_LEN = 512
N_SEQ = 4


def draw_attn_inputs(key, part):
    model_width = HEADS * HEAD_DIM
    full_shape = (CLIPS, CLIP_LEN, 3 * model_width)
    first_key = jax.random.fold_in(key, 0)
    column = lax.broadcasted_iota(jnp.int32, (1, 1, 3 * model_width), 2)
    normal_draw = jax.random.normal(first_key, full_shape, jnp.float32)
    factor = jnp.where(column < 2 * model_width, 1.22, 1.0)
    return jnp.clip(normal_draw * factor, -8.0, 8.0).astype(jnp.bfloat16)


def level_of(own_key, extent, cuts, smallest, high):
    loudness = 1.0
    for dim, parts in cuts:
        draws = jax.random.uniform(jax.random.fold_in(jax.random.fold_in(own_key, 6), dim), (parts,), jnp.float32, smallest / len(cuts), high / len(cuts))
        loudness = loudness * jnp.repeat(jnp.exp(draws), extent[dim] // parts).reshape((-1,) + (1,) * (len(extent) - 1 - dim))
    return loudness


def shared_out(own_key, own, number, rows, number_of, top, bound, slope):
    sequence = jax.random.permutation(own_key, number_of)
    crowded, common = load_shares(number_of, rows * top, bound, slope, True), load_shares(number_of, rows * top, bound, slope, False)
    places = jnp.arange(number_of)

    def named(lengths, rotation):
        used = int((lengths > 0).sum())
        fixed = max(1, used // 4)
        moved = fixed + (places - fixed + rotation * (used - fixed)) % max(1, number_of - fixed)
        return jnp.zeros((number_of,), jnp.int32).at[sequence[jnp.where(places < fixed, places, moved)]].set(jnp.asarray(lengths, jnp.int32))

    lengths = jnp.where(number % 4 == 0, named(crowded, number // 4), named(common, number - number // 4 - 1))
    mixed = jax.random.permutation(jax.random.fold_in(own, 3), number_of)
    giver, taker = mixed[0:number_of // 2 * 2:2], mixed[1:number_of // 2 * 2:2]
    margin = jnp.minimum(lengths[giver] - 1, bound - lengths[taker]) // 2
    margin = jnp.where((giver == sequence[0]) | (taker == sequence[0]) | (lengths[taker] == 0), 0, jnp.maximum(margin, 0))
    moved = jax.random.randint(jax.random.fold_in(own, 4), (number_of // 2,), 0, 1 << 20) % (margin + 1)
    lengths = lengths.at[giver].add(-moved).at[taker].add(moved)
    members = jnp.searchsorted(jnp.cumsum(lengths), jnp.arange(rows * top), side="right").astype(jnp.int32)
    grid = members.reshape(top, rows).T
    grid = grid[jax.random.permutation(jax.random.fold_in(own, 1), rows)]
    rotation = jax.random.randint(jax.random.fold_in(own, 2), (rows, 1), 0, top)
    return jnp.take_along_axis(grid, (jnp.arange(top)[None, :] + rotation) % top, axis=1)


def load_shares(count, total, most, lean, full):
    portions = [(1 << 20) // math.isqrt(rank ** lean) + 1 for rank in range(1, count + 1)]
    largest = most if full else min(most, max(-(-total // count), total * portions[0] // sum(portions)))
    least = 1 if total - largest >= count - 1 else 0
    holding, spare = [largest] + [least] * (count - 1), total - largest - least * (count - 1)
    while spare > 0:
        candidates = [i for i in range(1, count) if holding[i] < largest] or [i for i in range(1, count) if holding[i] < most]
        whole, remaining = sum([portions[i] for i in candidates]), spare
        for i in candidates:
            more = min(most - holding[i], max(1, remaining * portions[i] // whole), spare)
            holding[i] = holding[i] + more
            spare = spare - more
    return np.array(holding)


def bell_draw(rng, extent, width, limit, cuts=(), kind=jnp.bfloat16):
    drawn = jax.random.normal(rng, extent, jnp.float32) * width
    if len(cuts) > 0:
        drawn = level_of(rng, extent, cuts, -0.22, 0.18) * drawn
    return jnp.clip(drawn, min=-limit, max=limit).astype(kind)


def setup_inputs(seed: int = 0) -> dict:
    seeds = jax.random.split(jax.random.key(seed), 10)
    attn_inputs = draw_attn_inputs(jax.random.fold_in(seeds[9], 71), 0)
    residual = bell_draw(seeds[1], (CLIPS, CLIP_LEN, D), 1.0, 6.0, ((0, 32), (1, 4)))
    out_weight = bell_draw(seeds[2], (D, D), D ** -0.5, 0.125, ((0, 32),))
    norm_gain = jnp.clip(1.0 + 0.18 * jax.random.normal(seeds[3], (D,), jnp.float32), 0.1, 1.9)
    expert_ids_keys = jax.random.split(jax.random.fold_in(seeds[4], 1), CLIPS * CLIP_LEN // TOK_DEV)
    expert_ids_turns = jax.random.permutation(jax.random.fold_in(seeds[4], 3), CLIPS * CLIP_LEN // TOK_DEV)
    expert_ids = jax.vmap(lambda own, number: shared_out(jax.random.fold_in(seeds[4], 2), own, number, TOK_DEV, EXPERTS, TOP, CAP, 2))(expert_ids_keys, expert_ids_turns).reshape((CLIPS, CLIP_LEN, TOP))
    gate_weights = jnp.clip(0.1 + 0.9 * jax.random.uniform(seeds[5], (CLIPS, CLIP_LEN, TOP), jnp.float32) ** level_of(seeds[5], (CLIPS, CLIP_LEN, TOP), ((0, 32), (1, 4)), -0.2, 0.2), 0.1, 1.0)
    gate_weight = bell_draw(seeds[6], (EXPERTS, D, FF), D ** -0.5, 0.125, ((0, 32), (2, 4)))
    up_weight = bell_draw(seeds[7], (EXPERTS, D, FF), D ** -0.5, 0.125, ((0, 32), (2, 4)))
    down_weight = bell_draw(seeds[8], (EXPERTS, FF, D), FF ** -0.5, 0.078125, ((0, 32), (1, 4)))
    return {"attn_inputs": attn_inputs, "residual": residual, "out_weight": out_weight, "norm_gain": norm_gain, "expert_ids": expert_ids, "gate_weights": gate_weights, "gate_weight": gate_weight, "up_weight": up_weight, "down_weight": down_weight}


def attend_clip(clip_inputs):
    model_width = HEADS * HEAD_DIM
    query_rows = clip_inputs[:, :model_width].reshape(-1, HEADS, HEAD_DIM).astype(jnp.float32)
    key_rows = clip_inputs[:, model_width:2 * model_width].reshape(-1, HEADS, HEAD_DIM).astype(jnp.float32)
    value_rows = clip_inputs[:, 2 * model_width:].reshape(-1, HEADS, HEAD_DIM).astype(jnp.float32)
    scores = jnp.einsum('qhd,khd->hqk', query_rows, key_rows, precision=lax.Precision.HIGHEST) * HEAD_DIM ** (-0.5)
    attn_probs = jax.nn.softmax(scores, axis=-1).astype(jnp.bfloat16)
    mixed_heads = jnp.einsum('hqk,khd->qhd', attn_probs.astype(jnp.float32), value_rows, precision=lax.Precision.HIGHEST)
    return mixed_heads.astype(jnp.bfloat16).reshape(-1, model_width)

def expert_apply(operands):
    gate_mat, up_mat, down_mat, tok_rows = operands
    gate_val = jnp.dot(tok_rows, gate_mat, preferred_element_type=jnp.float32)
    up_val = jnp.dot(tok_rows, up_mat, preferred_element_type=jnp.float32)
    hidden = (jax.nn.silu(gate_val) * up_val).astype(jnp.bfloat16)
    quarter = FF // N_SEQ
    partial_terms = jnp.einsum('rsf,sfd->srd', hidden.reshape(-1, N_SEQ, quarter).astype(jnp.float32), down_mat.reshape(N_SEQ, quarter, -1).astype(jnp.float32), precision=lax.Precision.HIGHEST)
    rounded = lax.optimization_barrier(partial_terms.astype(jnp.bfloat16))
    return lax.optimization_barrier(jnp.sum(rounded.astype(jnp.float32), axis=0)).astype(jnp.bfloat16)

def reference(attn_inputs, residual, out_weight, norm_gain, expert_ids, gate_weights, gate_weight, up_weight, down_weight):
    model_width = residual.shape[-1]
    attended = lax.map(attend_clip, attn_inputs)
    projected = jnp.dot(attended.reshape(-1, model_width), out_weight, preferred_element_type=jnp.float32)
    middle = lax.optimization_barrier((residual.reshape(-1, model_width).astype(jnp.float32) + projected).astype(jnp.bfloat16))
    mid_float = middle.astype(jnp.float32)
    normed = (mid_float * lax.rsqrt(lax.optimization_barrier(jnp.mean(mid_float * mid_float, axis=-1, keepdims=True)) + 1e-06) * norm_gain).astype(jnp.bfloat16)
    blocks = CLIPS * N_SEQ
    route_ids = expert_ids.reshape(blocks, TOK_DEV * TOP).astype(jnp.int32)
    one_hot = (route_ids[:, :, None] == jnp.arange(EXPERTS, dtype=jnp.int32)[None, None, :]).astype(jnp.int32)
    before = (jnp.cumsum(one_hot, axis=1).astype(jnp.int32) - one_hot).astype(jnp.int32)
    slot_ids = lax.optimization_barrier(jnp.sum(before * one_hot, axis=-1)).astype(jnp.int32)
    block_ids = jnp.broadcast_to(jnp.arange(blocks, dtype=jnp.int32)[:, None], route_ids.shape).astype(jnp.int32)
    flat_index = ((block_ids * EXPERTS + route_ids) * CAP + slot_ids).astype(jnp.int32)
    buffer = jnp.zeros((blocks * EXPERTS * CAP, model_width), jnp.bfloat16).at[flat_index.reshape(-1)].set(jnp.repeat(normed, TOP, axis=0))
    expert_in = buffer.reshape(blocks, EXPERTS, CAP, model_width).transpose(1, 0, 2, 3).reshape(EXPERTS, blocks * CAP, model_width)
    expert_out = lax.map(expert_apply, (gate_weight, up_weight, down_weight, expert_in)).reshape(EXPERTS, blocks, CAP, model_width)
    picked = expert_out[route_ids, block_ids, slot_ids]
    weighted = picked.astype(jnp.float32).reshape(-1, TOP, model_width) * gate_weights.reshape(-1, TOP, 1).astype(jnp.float32)
    result = mid_float + lax.optimization_barrier(jnp.sum(weighted, axis=1))
    return result.astype(jnp.bfloat16).reshape(CLIPS, CLIP_LEN, model_width)
```

```python
import functools

import jax
import jax.numpy as jnp
from jax import lax
from jax.experimental import pallas as pl
from jax.experimental.pallas import tpu as pltpu
from jax.sharding import PartitionSpec as P

HEADS = 16
HEAD_DIM = 128
TOP = 2
TOK = 128
D = 2048
FFL = 1408
EXPERTS = 32
MESH = pl.DeviceIdType.MESH
BF = jnp.bfloat16
F32 = jnp.float32
MAIN = 8
GROUPS = 4
QUART = D // 4


def attend_block(query_block, key_rows, value_rows):
    scores = jnp.einsum(
        "qhd,khd->hqk", query_block, key_rows, preferred_element_type=jnp.float32
    ) * HEAD_DIM ** (-0.5)
    attn_probs = jax.nn.softmax(scores, axis=-1).astype(jnp.bfloat16)
    mixed_heads = jnp.einsum(
        "hqk,khd->qhd", attn_probs, value_rows, preferred_element_type=jnp.float32
    )
    return mixed_heads.astype(jnp.bfloat16)


def position():
    s = lax.axis_index("seq")
    e = lax.axis_index("exp")
    return s, lax.rem(lax.div(e, 8), 4), lax.rem(lax.div(e, 2), 4), lax.rem(e, 2)


def plane_device(s, y, x, c, i, sign):
    dy, dx, dc = lax.div(i, 8), lax.rem(lax.div(i, 2), 4), lax.rem(i, 2)
    ny = lax.rem(y + sign * dy + 4, 4)
    nx = lax.rem(x + sign * dx + 4, 4)
    nc = lax.rem(c + dc, 2)
    return (s, (ny * 4 + nx) * 2 + nc)


def rel_index(ids, y, x, c):
    dy = ((ids >> 3) + (4 - y)) & 3
    dx = (((ids >> 1) & 3) + (4 - x)) & 3
    dc = ((ids & 1) + c) & 1
    return dy * 8 + dx * 2 + dc


def onehot(cond):
    return jnp.where(cond, 1.0, 0.0)


def split_slot(rel, slot):
    main = jnp.where(slot < MAIN, rel * MAIN + slot, -1)
    tail = jnp.where(slot >= MAIN, rel * 2 + slot - MAIN, -1)
    return main, tail


def routes_cols(ids, y, x, c):
    lane = lax.broadcasted_iota(jnp.int32, (TOK, EXPERTS), 1)
    hot = [onehot(lane == ids[:, k : k + 1]) for k in range(TOP)]
    row = lax.broadcasted_iota(jnp.int32, (TOK, TOK), 0)
    col = lax.broadcasted_iota(jnp.int32, (TOK, TOK), 1)
    before = jnp.dot(
        onehot(col < row).astype(BF), (hot[0] + hot[1]).astype(BF), preferred_element_type=F32
    )
    out = []
    for k in range(TOP):
        slot = jnp.sum(hot[k] * before, axis=1, keepdims=True).astype(jnp.int32)
        out.append(split_slot(rel_index(ids[:, k : k + 1], y, x, c), slot))
    return out


def routes_rows(ids, y, x, c):
    sub = lax.broadcasted_iota(jnp.int32, (EXPERTS, TOK), 0)
    hot = [onehot(sub == ids[k : k + 1, :]) for k in range(TOP)]
    row = lax.broadcasted_iota(jnp.int32, (TOK, TOK), 0)
    col = lax.broadcasted_iota(jnp.int32, (TOK, TOK), 1)
    before = jnp.dot(
        (hot[0] + hot[1]).astype(BF), onehot(row < col).astype(BF), preferred_element_type=F32
    )
    out = []
    for k in range(TOP):
        slot = jnp.sum(hot[k] * before, axis=0, keepdims=True).astype(jnp.int32)
        out.append(split_slot(rel_index(ids[k : k + 1, :], y, x, c), slot))
    return out


def expert_kernel(
    normed,
    mid,
    ids,
    ids_t,
    gates,
    wg_hbm,
    wu_hbm,
    wd_hbm,
    out,
    wg,
    wu,
    wd,
    send_m,
    send_f,
    recv_m,
    recv_f,
    hid,
    part_m,
    part_f,
    far_m,
    far_f,
    sum_m,
    sum_f,
    near_m,
    near_f,
    red_m,
    red_f,
    back_m,
    back_f,
    w_sem,
    ip_s,
    ip_r,
    f_s,
    f_r,
    r_s,
    r_r,
    a_s,
    a_r,
    b_s,
    b_r,
    c_s,
    c_r,
    o_s,
    o_r,
):
    s, y, x, c = position()
    exp_me = (y * 4 + x) * 2 + c
    up = (lax.rem(s + 1, 4), exp_me)
    down = (lax.rem(s + 3, 4), exp_me)
    zdev = (up, down)

    def remote(src, dst, ss, rs, dev):
        return pltpu.make_async_remote_copy(
            src_ref=src, dst_ref=dst, send_sem=ss, recv_sem=rs, device_id=dev, device_id_type=MESH
        )

    barrier = pltpu.get_barrier_semaphore()

    @pl.loop(1, 32)
    def _(i):
        pl.semaphore_signal(
            barrier, inc=1, device_id=plane_device(s, y, x, c, i, 1), device_id_type=MESH
        )

    for dev in zdev:
        pl.semaphore_signal(barrier, inc=1, device_id=dev, device_id_type=MESH)

    loads = [
        pltpu.make_async_copy(h, v, w_sem.at[i])
        for i, (h, v) in enumerate(((wg_hbm, wg), (wu_hbm, wu), (wd_hbm, wd)))
    ]
    for ld in loads:
        ld.start()

    rows = routes_rows(ids_t[...], y, x, c)
    sub = lax.broadcasted_iota(jnp.int32, (EXPERTS * MAIN, TOK), 0)
    place = onehot((sub == rows[0][0]) | (sub == rows[1][0])).astype(BF)
    fold_place = [
        onehot((sub == rows[0][1] * 4 + k) | (sub == rows[1][1] * 4 + k)).astype(BF)
        for k in range(4)
    ]
    fold = None
    for k in range(4):
        cols = slice(k * QUART, (k + 1) * QUART)
        tokens = normed[:, cols]
        send_m[:, cols] = jnp.dot(place, tokens, preferred_element_type=F32).astype(BF)
        term = jnp.dot(fold_place[k], tokens, preferred_element_type=F32)
        fold = term if fold is None else fold + term
    send_f[...] = fold.astype(BF)
    recv_m[0, 0:MAIN, :] = send_m[0:MAIN, :]
    recv_f[0, 0:MAIN, :] = send_f[0:MAIN, :]

    pl.semaphore_wait(barrier, 33)

    def inplane(i):
        dev = plane_device(s, y, x, c, i, 1)
        g, k = lax.div(i, 8), lax.rem(i, 8)
        src = pl.ds(pl.multiple_of(i * MAIN, MAIN), MAIN)
        dst = pl.ds(pl.multiple_of(k * MAIN, MAIN), MAIN)
        return (
            remote(send_m.at[src], recv_m.at[g, dst], ip_s.at[i, 0], ip_r.at[i, 0], dev),
            remote(send_f.at[src], recv_f.at[g, dst], ip_s.at[i, 1], ip_r.at[i, 1], dev),
        )

    @pl.loop(1, 32)
    def _(i):
        for cp in inplane(i):
            cp.start()

    def ranges(size, off):
        return pl.ds(off, size)

    def pair(src_m, src_f, srow, dst_m, dst_f, drow, ss, rs, dev):
        return (
            remote(src_m.at[srow], dst_m.at[drow], ss.at[0], rs.at[0], dev),
            remote(src_f.at[srow], dst_f.at[drow], ss.at[1], rs.at[1], dev),
        )

    def forward(g, d):
        drow = ranges(64, 192 if d == 0 else 64)
        return pair(
            recv_m.at[g], recv_f.at[g], ranges(64, 0), recv_m.at[g], recv_f.at[g], drow,
            f_s.at[g, d], f_r.at[g, d], zdev[d],
        )

    def relay(g, d):
        srow = ranges(32, 192 if d == 0 else 96)
        drow = ranges(32, 128 if d == 0 else 160)
        return pair(
            recv_m.at[g], recv_f.at[g], srow, recv_m.at[g], recv_f.at[g], drow,
            r_s.at[g, d], r_r.at[g, d], zdev[d],
        )

    def far(g, d):
        srow = ranges(32, 128 if d == 0 else 160)
        return pair(
            part_m.at[g], part_f.at[g], srow, far_m.at[g, d], far_f.at[g, d], ranges(32, 0),
            a_s.at[g, d], a_r.at[g, d], zdev[d],
        )

    def direct(g, d):
        srow = ranges(32, 96 if d == 0 else 192)
        drow = ranges(32, 32 if d == 0 else 0)
        return pair(
            part_m.at[g], part_f.at[g], srow, near_m.at[g, d], near_f.at[g, d], drow,
            b_s.at[g, d], b_r.at[g, d], zdev[d],
        )

    def summed(g, d):
        drow = ranges(32, 0 if d == 0 else 32)
        return pair(
            sum_m.at[g, d], sum_f.at[g, d], ranges(32, 0), near_m.at[g, d], near_f.at[g, d], drow,
            c_s.at[g, d], c_r.at[g, d], zdev[d],
        )

    def home(g, k):
        i = g * 8 + k
        dev = plane_device(s, y, x, c, i, -1)
        src = pl.ds(pl.multiple_of(k * MAIN, MAIN), MAIN)
        dst = pl.ds(pl.multiple_of(i * MAIN, MAIN), MAIN)
        return (
            remote(red_m.at[g, src], back_m.at[dst], o_s.at[i, 0], o_r.at[i, 0], dev),
            remote(red_f.at[g, src], back_f.at[dst], o_s.at[i, 1], o_r.at[i, 1], dev),
        )

    def start(make, g):
        for d in range(2):
            for cp in make(g, d):
                cp.start()

    def arrived(make, g):
        for d in range(2):
            for cp in make(g, d):
                cp.wait_recv()

    def dispatch_group(g):
        @pl.loop(max(1, g * 8), g * 8 + 8)
        def _(i):
            for cp in inplane(i):
                cp.wait_recv()

        start(forward, g)

    def relay_group(g):
        arrived(forward, g)
        start(relay, g)

    perm_row = lax.broadcasted_iota(jnp.int32, (256, 256), 0)
    perm_col = lax.broadcasted_iota(jnp.int32, (256, 256), 1)

    def experts(g):
        arrived(relay, g)
        unfold = onehot(perm_col == (perm_row & 63) * 4 + (perm_row >> 6)).astype(BF)
        tail = jnp.dot(unfold, recv_f[g], preferred_element_type=F32).astype(BF)
        for k in range(4):
            recv_m[g, 256:320, k * QUART : (k + 1) * QUART] = tail[k * 64 : (k + 1) * 64, :]

        def hidden(cols):
            gate = jnp.dot(recv_m[g], wg[:, cols], preferred_element_type=F32)
            upv = jnp.dot(recv_m[g], wu[:, cols], preferred_element_type=F32)
            hid[:, cols] = (gate / (1.0 + jnp.exp(-gate)) * upv).astype(BF)

        @pl.loop(0, 5)
        def _(j):
            hidden(pl.ds(pl.multiple_of(j * 256, 256), 256))

        hidden(pl.ds(1280, 128))

        @pl.loop(0, 8)
        def _(j):
            cols = pl.ds(pl.multiple_of(j * 256, 256), 256)
            part_m[g, :, cols] = jnp.dot(
                hid[...], wd[:, cols], preferred_element_type=F32
            ).astype(BF)

        fold_back = onehot(perm_row == (perm_col & 63) * 4 + (perm_col >> 6)).astype(BF)
        stacked = jnp.concatenate(
            [part_m[g, 256:320, k * QUART : (k + 1) * QUART] for k in range(4)], axis=0
        )
        part_f[g] = jnp.dot(fold_back, stacked, preferred_element_type=F32).astype(BF)
        start(far, g)
        start(direct, g)

    def pass_sums(g):
        arrived(far, g)
        for d in range(2):
            own = pl.ds(64 if d == 0 else 224, 32)
            sum_m[g, d] = (part_m[g, own, :].astype(F32) + far_m[g, d].astype(F32)).astype(BF)
            sum_f[g, d] = (part_f[g, own, :].astype(F32) + far_f[g, d].astype(F32)).astype(BF)
        start(summed, g)

    def go_home(g):
        arrived(direct, g)
        arrived(summed, g)
        red_m[g] = (
            part_m[g, 0:64, :].astype(F32) + near_m[g, 0].astype(F32) + near_m[g, 1].astype(F32)
        ).astype(BF)
        red_f[g] = (
            part_f[g, 0:64, :].astype(F32) + near_f[g, 0].astype(F32) + near_f[g, 1].astype(F32)
        ).astype(BF)
        if g == 0:
            back_m[0:MAIN, :] = red_m[0, 0:MAIN, :]
            back_f[0:MAIN, :] = red_f[0, 0:MAIN, :]

        @pl.loop(1 if g == 0 else 0, 8)
        def _(k):
            for cp in home(g, k):
                cp.start()

    dispatch_group(0)
    dispatch_group(1)
    relay_group(0)
    dispatch_group(2)
    relay_group(1)
    dispatch_group(3)
    for ld in loads:
        ld.wait()
    experts(0)
    relay_group(2)
    experts(1)
    pass_sums(0)
    relay_group(3)
    experts(2)
    pass_sums(1)
    go_home(0)
    experts(3)
    pass_sums(2)
    go_home(1)
    pass_sums(3)
    go_home(2)
    go_home(3)

    cols_of = routes_cols(ids[...], y, x, c)
    lane = lax.broadcasted_iota(jnp.int32, (TOK, EXPERTS * MAIN), 1)

    @pl.loop(1, 32)
    def _(i):
        for cp in home(lax.div(i, 8), lax.rem(i, 8)):
            cp.wait_recv()

    for k in range(4):
        cols = slice(k * QUART, (k + 1) * QUART)
        total = mid[:, cols].astype(F32)
        for ch in range(TOP):
            main, tail = cols_of[ch]
            picked = jnp.dot(
                onehot(lane == main).astype(BF), back_m[:, cols], preferred_element_type=F32
            ) + jnp.dot(
                onehot(lane == tail * 4 + k).astype(BF), back_f[...], preferred_element_type=F32
            )
            total = total + picked * gates[:, ch : ch + 1]
        out[:, cols] = total.astype(BF)

    @pl.loop(1, 32)
    def _(i):
        for cp in inplane(i):
            cp.wait_send()
        for cp in home(lax.div(i, 8), lax.rem(i, 8)):
            cp.wait_send()

    for g in range(GROUPS):
        for make in (forward, relay, far, direct, summed):
            for d in range(2):
                for cp in make(g, d):
                    cp.wait_send()


def expert_stage(normed, middle, ids, gates, wg, wu, wd):
    vm = pl.BlockSpec(memory_space=pltpu.VMEM)
    hb = pl.BlockSpec(memory_space=pl.ANY)
    dma = pltpu.SemaphoreType.DMA
    G = GROUPS
    scratch = [
        pltpu.VMEM((D, FFL), BF),
        pltpu.VMEM((D, FFL), BF),
        pltpu.VMEM((FFL, D), BF),
        pltpu.VMEM((256, D), BF),
        pltpu.VMEM((256, QUART), BF),
        pltpu.VMEM((G, 320, D), BF),
        pltpu.VMEM((G, 256, QUART), BF),
        pltpu.VMEM((320, FFL), BF),
        pltpu.VMEM((G, 320, D), BF),
        pltpu.VMEM((G, 256, QUART), BF),
        pltpu.VMEM((G, 2, 32, D), BF),
        pltpu.VMEM((G, 2, 32, QUART), BF),
        pltpu.VMEM((G, 2, 32, D), BF),
        pltpu.VMEM((G, 2, 32, QUART), BF),
        pltpu.VMEM((G, 2, 64, D), BF),
        pltpu.VMEM((G, 2, 64, QUART), BF),
        pltpu.VMEM((G, 64, D), BF),
        pltpu.VMEM((G, 64, QUART), BF),
        pltpu.VMEM((256, D), BF),
        pltpu.VMEM((256, QUART), BF),
        dma((3,)),
        dma((32, 2)),
        dma((32, 2)),
    ]
    scratch += [dma((G, 2, 2)) for _ in range(10)]
    scratch += [dma((32, 2)), dma((32, 2))]
    return pl.pallas_call(
        expert_kernel,
        out_shape=jax.ShapeDtypeStruct((TOK, D), BF),
        in_specs=[vm] * 5 + [hb] * 3,
        out_specs=vm,
        scratch_shapes=scratch,
        name="expert_stage",
        compiler_params=pltpu.CompilerParams(
            collective_id=0, has_side_effects=True, vmem_limit_bytes=60 * 2**20
        ),
    )(normed, middle, ids, ids.T, gates, wg, wu, wd)


def per_device(
    attn_inputs,
    residual,
    out_weight,
    norm_gain,
    expert_ids,
    gate_weights,
    gate_weight,
    up_weight,
    down_weight,
):
    tok_count = attn_inputs.shape[1]
    seq_count = lax.axis_size("seq")
    model_width = residual.shape[-1]
    head_local = HEADS // seq_count
    laid = attn_inputs.reshape(tok_count, 3, seq_count, head_local * HEAD_DIM)
    by_heads = lax.all_to_all(laid, "seq", split_axis=2, concat_axis=0, tiled=True)
    clip_len = by_heads.shape[0]
    queries = by_heads[:, 0, 0].reshape(clip_len, head_local, HEAD_DIM)
    keys_all = by_heads[:, 1, 0].reshape(clip_len, head_local, HEAD_DIM)
    values_all = by_heads[:, 2, 0].reshape(clip_len, head_local, HEAD_DIM)
    attended = attend_block(queries, keys_all, values_all)
    attended = attended.reshape(clip_len, head_local * HEAD_DIM)
    merged = lax.all_to_all(attended, "seq", split_axis=0, concat_axis=1, tiled=True)
    projected = jnp.dot(
        merged,
        lax.all_gather(out_weight, "exp", axis=0, tiled=True),
        preferred_element_type=jnp.float32,
    )
    middle = lax.optimization_barrier(
        (residual.reshape(tok_count, model_width).astype(jnp.float32) + projected).astype(
            jnp.bfloat16
        )
    )
    mid_float = middle.astype(jnp.float32)
    normed = (
        mid_float
        * lax.rsqrt(jnp.mean(mid_float * mid_float, axis=-1, keepdims=True) + 1e-06)
        * norm_gain
    ).astype(jnp.bfloat16)
    result = expert_stage(
        normed,
        middle,
        expert_ids.reshape(tok_count, TOP),
        gate_weights.reshape(tok_count, TOP),
        gate_weight[0],
        up_weight[0],
        down_weight[0],
    )
    return result.reshape(1, tok_count, model_width)


def solution(mesh):
    placed = (
        P("exp", "seq", None),
        P("exp", "seq", None),
        P("exp", None),
        P(),
        P("exp", "seq", None),
        P("exp", "seq", None),
        P("exp", None, "seq"),
        P("exp", None, "seq"),
        P("exp", "seq", None),
    )
    return jax.shard_map(
        per_device, mesh=mesh, in_specs=placed, out_specs=P("exp", "seq", None), check_vma=False
    )
```

```python
import jax
import jax.numpy as jnp
from jax import lax
from jax.experimental import pallas as pl
from jax.experimental.pallas import tpu as pltpu
from jax.sharding import PartitionSpec as P

HEADS = 16
HEAD_DIM = 128
TOP = 2
TOK = 128
D = 2048
FFL = 1408
EXPERTS = 32
MESH = pl.DeviceIdType.MESH
BF = jnp.bfloat16
F32 = jnp.float32
MAIN = 8
GROUPS = 4
QUART = D // 4


def position():
    s = lax.axis_index("seq")
    e = lax.axis_index("exp")
    return s, lax.rem(lax.div(e, 8), 4), lax.rem(lax.div(e, 2), 4), lax.rem(e, 2)


def plane_device(s, y, x, c, i, sign):
    dy, dx, dc = lax.div(i, 8), lax.rem(lax.div(i, 2), 4), lax.rem(i, 2)
    ny = lax.rem(y + sign * dy + 4, 4)
    nx = lax.rem(x + sign * dx + 4, 4)
    nc = lax.rem(c + dc, 2)
    return (s, (ny * 4 + nx) * 2 + nc)


def rel_index(ids, y, x, c):
    dy = ((ids >> 3) + (4 - y)) & 3
    dx = (((ids >> 1) & 3) + (4 - x)) & 3
    dc = ((ids & 1) + c) & 1
    return dy * 8 + dx * 2 + dc


def onehot(cond):
    return jnp.where(cond, 1.0, 0.0)


def split_slot(rel, slot):
    main = jnp.where(slot < MAIN, rel * MAIN + slot, -1)
    tail = jnp.where(slot >= MAIN, rel * 2 + slot - MAIN, -1)
    return main, tail


def routes_cols(ids, y, x, c):
    lane = lax.broadcasted_iota(jnp.int32, (TOK, EXPERTS), 1)
    hot = [onehot(lane == ids[:, k : k + 1]) for k in range(TOP)]
    row = lax.broadcasted_iota(jnp.int32, (TOK, TOK), 0)
    col = lax.broadcasted_iota(jnp.int32, (TOK, TOK), 1)
    before = jnp.dot(
        onehot(col < row).astype(BF), (hot[0] + hot[1]).astype(BF), preferred_element_type=F32
    )
    out = []
    for k in range(TOP):
        slot = jnp.sum(hot[k] * before, axis=1, keepdims=True).astype(jnp.int32)
        out.append(split_slot(rel_index(ids[:, k : k + 1], y, x, c), slot))
    return out


def routes_rows(ids, y, x, c):
    sub = lax.broadcasted_iota(jnp.int32, (EXPERTS, TOK), 0)
    hot = [onehot(sub == ids[k : k + 1, :]) for k in range(TOP)]
    row = lax.broadcasted_iota(jnp.int32, (TOK, TOK), 0)
    col = lax.broadcasted_iota(jnp.int32, (TOK, TOK), 1)
    before = jnp.dot(
        (hot[0] + hot[1]).astype(BF), onehot(row < col).astype(BF), preferred_element_type=F32
    )
    out = []
    for k in range(TOP):
        slot = jnp.sum(hot[k] * before, axis=0, keepdims=True).astype(jnp.int32)
        out.append(split_slot(rel_index(ids[k : k + 1, :], y, x, c), slot))
    return out


def layer_kernel(
    qkv_hbm,
    resid,
    ow_hbm,
    gain,
    ids,
    ids_t,
    gates,
    wg_hbm,
    wu_hbm,
    wd_hbm,
    out,
    qkv,
    att,
    merged,
    ow,
    normed,
    mid,
    wg,
    wu,
    wd,
    send_m,
    send_f,
    recv_m,
    recv_f,
    hid,
    part_m,
    part_f,
    far_m,
    far_f,
    sum_m,
    sum_f,
    near_m,
    near_f,
    red_m,
    red_f,
    back_m,
    back_f,
    l_sem,
    q_s,
    q_r,
    h_s,
    h_r,
    x_s,
    x_r,
    t_s,
    t_r,
    w_sem,
    ip_s,
    ip_r,
    f_s,
    f_r,
    r_s,
    r_r,
    a_s,
    a_r,
    b_s,
    b_r,
    c_s,
    c_r,
    o_s,
    o_r,
):
    s, y, x, c = position()
    exp_me = (y * 4 + x) * 2 + c
    up = (lax.rem(s + 1, 4), exp_me)
    down = (lax.rem(s + 3, 4), exp_me)
    zdev = (up, down)
    across = (lax.rem(s + 2, 4), exp_me)

    def remote(src, dst, ss, rs, dev):
        return pltpu.make_async_remote_copy(
            src_ref=src, dst_ref=dst, send_sem=ss, recv_sem=rs, device_id=dev, device_id_type=MESH
        )

    barrier = pltpu.get_barrier_semaphore()

    @pl.loop(1, 32)
    def _(i):
        pl.semaphore_signal(
            barrier, inc=1, device_id=plane_device(s, y, x, c, i, 1), device_id_type=MESH
        )

    for dev in (up, down, across):
        pl.semaphore_signal(barrier, inc=1, device_id=dev, device_id_type=MESH)

    loads = [
        pltpu.make_async_copy(h, v, w_sem.at[i])
        for i, (h, v) in enumerate(((wg_hbm, wg), (wu_hbm, wu), (wd_hbm, wd)))
    ]
    for ld in loads:
        ld.start()

    own_cols = pl.multiple_of(s * 512, 512)
    chip_row = (y * 4 + x) * 128
    own_ow = pl.ds(pl.multiple_of(chip_row + c * 64, 64), 64)
    local = [
        pltpu.make_async_copy(
            qkv_hbm.at[:, pl.ds(pl.multiple_of(own_cols + p * D, 512), 512)],
            qkv.at[p, pl.ds(0, TOK)],
            l_sem.at[p],
        )
        for p in range(3)
    ]
    local.append(pltpu.make_async_copy(ow_hbm, ow.at[own_ow], l_sem.at[3]))
    for ld in local:
        ld.start()

    def seq_peer(r):
        return (lax.rem(s + r, 4), exp_me)

    def send_head(h, r, p):
        cols = pl.multiple_of(lax.rem(s + r, 4) * 512 + (p * D + h * HEAD_DIM), HEAD_DIM)
        return remote(
            qkv_hbm.at[:, pl.ds(cols, HEAD_DIM)],
            qkv.at[p, pl.ds((4 - r) * TOK, TOK), pl.ds(h * HEAD_DIM, HEAD_DIM)],
            q_s.at[h, r - 1, p],
            q_r.at[h, r - 1, p],
            seq_peer(r),
        )

    def return_head(h, r):
        cols = pl.ds(h * HEAD_DIM, HEAD_DIM)
        return remote(
            att.at[r, :, cols],
            merged.at[4 - r, :, cols],
            h_s.at[h, r - 1],
            h_r.at[h, r - 1],
            seq_peer(r),
        )

    half_cols = pl.ds(pl.multiple_of(c * 1024, 1024), 1024)

    def chip_at(a, b):
        ny = lax.rem(y + (1 - c) * b + c * a, 4)
        nx = lax.rem(x + (1 - c) * a + c * b, 4)
        return ny * 4 + nx

    def chunk(a, b, part=None):
        base = chip_at(a, b) * 128
        size = 128
        if part is not None:
            base, size = base + part * 64, 64
        return ow.at[pl.ds(pl.multiple_of(base, 64), size), half_cols]

    def ring_device(axis, step):
        other = chip_at(step, 0) if axis == 0 else chip_at(0, step)
        return (s, other * 2 + c)

    partner = (s, (y * 4 + x) * 2 + 1 - c)

    def ring(axis, a, d):
        ref = chunk(0, 0) if axis == 0 else chunk(a, 0)
        at = 4 if axis == 0 else a
        return remote(
            ref, ref, x_s.at[at, d, 0], x_r.at[at, d, 0], ring_device(axis, 1 if d == 0 else 3)
        )

    def ring_relay(axis, a, d):
        o = 3 if d == 0 else 1
        ref = chunk(o, 0, d) if axis == 0 else chunk(a, o, d)
        at = 4 if axis == 0 else a
        return remote(
            ref, ref, x_s.at[at, d, 1], x_r.at[at, d, 1], ring_device(axis, 1 if d == 0 else 3)
        )

    def swap_chip():
        ref = ow.at[own_ow]
        return remote(ref, ref, t_s.at[0], t_r.at[0], partner)

    def swap(a, b):
        ref = chunk(a, b)
        return remote(ref, ref, t_s.at[a * 4 + b], t_r.at[a * 4 + b], partner)

    pl.semaphore_wait(barrier, 34)

    @pl.loop(0, 4)
    def _(h):
        for r in (2, 1, 3):
            for p in range(3):
                send_head(h, r, p).start()

    local[3].wait()
    swap_chip().start()
    swap_chip().wait_recv()
    for d in range(2):
        ring(0, 0, d).start()
    for d in range(2):
        ring(1, 0, d).start()

    def first_axis():
        for d in range(2):
            ring(0, 0, d).wait_recv()
            ring_relay(0, 0, d).start()
        for a in (1, 3):
            for d in range(2):
                ring(1, a, d).start()
        for a in (1, 3):
            swap(a, 0).start()

    def first_axis_far():
        for d in range(2):
            ring_relay(0, 0, d).wait_recv()
        for d in range(2):
            ring(1, 2, d).start()
        swap(2, 0).start()

    def second_axis(a):
        for d in range(2):
            ring(1, a, d).wait_recv()
            ring_relay(1, a, d).start()
        for b in (1, 3):
            swap(a, b).start()

    def second_axis_far(a):
        for d in range(2):
            ring_relay(1, a, d).wait_recv()
        swap(a, 2).start()

    scale = HEAD_DIM ** (-0.5) * 1.4426950408889634

    def attend(h):
        for r in (2, 1, 3):
            for p in range(3):
                send_head(h, r, p).wait_recv()
        cols = slice(h * HEAD_DIM, (h + 1) * HEAD_DIM)

        @pl.loop(0, 4)
        def _(i):
            r = lax.rem(i + 1, 4)
            q = qkv[0, pl.ds(pl.multiple_of(r * TOK, TOK), TOK), cols]
            scores = lax.dot_general(
                q, qkv[1, :, cols], (((1,), (1,)), ((), ())), preferred_element_type=F32
            )
            top = jnp.max(scores, axis=1, keepdims=True)
            probs = jnp.exp2((scores - top) * scale)
            norm = jnp.sum(probs, axis=1, keepdims=True)
            mixed = jnp.dot(probs.astype(BF), qkv[2, :, cols], preferred_element_type=F32)
            att[r, :, cols] = (mixed / norm).astype(BF)

        for r in (2, 1, 3):
            return_head(h, r).start()

    for ld in local[:3]:
        ld.wait()
    first_axis()
    attend(0)
    second_axis(0)
    attend(1)
    first_axis_far()
    attend(2)
    second_axis(1)
    second_axis(3)
    attend(3)
    second_axis(2)
    merged[0] = att[0]
    for a in (0, 1, 3, 2):
        second_axis_far(a)
    for i in range(1, 16):
        swap(i // 4, i % 4).wait_recv()
    for h in range(4):
        for r in (2, 1, 3):
            return_head(h, r).wait_recv()

    square = jnp.zeros((TOK, 1), F32)
    for n in range(4):
        cols = slice(n * 512, (n + 1) * 512)
        acc = resid[:, cols].astype(F32)
        for j in range(4):
            rows_j = pl.ds(pl.multiple_of(lax.rem(s + j, 4) * 512, 512), 512)
            acc = acc + jnp.dot(merged[j], ow[rows_j, cols], preferred_element_type=F32)
        rounded = acc.astype(BF)
        mid[:, cols] = rounded
        wide = rounded.astype(F32)
        square = square + jnp.sum(wide * wide, axis=1, keepdims=True)
    inv = lax.rsqrt(square / D + 1e-06)
    for n in range(4):
        cols = slice(n * 512, (n + 1) * 512)
        normed[:, cols] = (mid[:, cols].astype(F32) * inv * gain[:, cols]).astype(BF)

    rows = routes_rows(ids_t[...], y, x, c)
    sub = lax.broadcasted_iota(jnp.int32, (EXPERTS * MAIN, TOK), 0)
    place = onehot((sub == rows[0][0]) | (sub == rows[1][0])).astype(BF)
    fold_place = [
        onehot((sub == rows[0][1] * 4 + k) | (sub == rows[1][1] * 4 + k)).astype(BF)
        for k in range(4)
    ]
    fold = None
    for k in range(4):
        cols = slice(k * QUART, (k + 1) * QUART)
        tokens = normed[:, cols]
        send_m[:, cols] = jnp.dot(place, tokens, preferred_element_type=F32).astype(BF)
        term = jnp.dot(fold_place[k], tokens, preferred_element_type=F32)
        fold = term if fold is None else fold + term
    send_f[...] = fold.astype(BF)
    recv_m[0, 0:MAIN, :] = send_m[0:MAIN, :]
    recv_f[0, 0:MAIN, :] = send_f[0:MAIN, :]

    def inplane(i):
        dev = plane_device(s, y, x, c, i, 1)
        g, k = lax.div(i, 8), lax.rem(i, 8)
        src = pl.ds(pl.multiple_of(i * MAIN, MAIN), MAIN)
        dst = pl.ds(pl.multiple_of(k * MAIN, MAIN), MAIN)
        return (
            remote(send_m.at[src], recv_m.at[g, dst], ip_s.at[i, 0], ip_r.at[i, 0], dev),
            remote(send_f.at[src], recv_f.at[g, dst], ip_s.at[i, 1], ip_r.at[i, 1], dev),
        )

    @pl.loop(1, 32)
    def _(i):
        for cp in inplane(i):
            cp.start()

    def ranges(size, off):
        return pl.ds(off, size)

    def pair(src_m, src_f, srow, dst_m, dst_f, drow, ss, rs, dev):
        return (
            remote(src_m.at[srow], dst_m.at[drow], ss.at[0], rs.at[0], dev),
            remote(src_f.at[srow], dst_f.at[drow], ss.at[1], rs.at[1], dev),
        )

    def forward(g, d):
        drow = ranges(64, 192 if d == 0 else 64)
        return pair(
            recv_m.at[g], recv_f.at[g], ranges(64, 0), recv_m.at[g], recv_f.at[g], drow,
            f_s.at[g, d], f_r.at[g, d], zdev[d],
        )

    def relay(g, d):
        srow = ranges(32, 192 if d == 0 else 96)
        drow = ranges(32, 128 if d == 0 else 160)
        return pair(
            recv_m.at[g], recv_f.at[g], srow, recv_m.at[g], recv_f.at[g], drow,
            r_s.at[g, d], r_r.at[g, d], zdev[d],
        )

    def far(g, d):
        srow = ranges(32, 128 if d == 0 else 160)
        return pair(
            part_m.at[g], part_f.at[g], srow, far_m.at[g, d], far_f.at[g, d], ranges(32, 0),
            a_s.at[g, d], a_r.at[g, d], zdev[d],
        )

    def direct(g, d):
        srow = ranges(32, 96 if d == 0 else 192)
        drow = ranges(32, 32 if d == 0 else 0)
        return pair(
            part_m.at[g], part_f.at[g], srow, near_m.at[g, d], near_f.at[g, d], drow,
            b_s.at[g, d], b_r.at[g, d], zdev[d],
        )

    def summed(g, d):
        drow = ranges(32, 0 if d == 0 else 32)
        return pair(
            sum_m.at[g, d], sum_f.at[g, d], ranges(32, 0), near_m.at[g, d], near_f.at[g, d], drow,
            c_s.at[g, d], c_r.at[g, d], zdev[d],
        )

    def home(g, k):
        i = g * 8 + k
        dev = plane_device(s, y, x, c, i, -1)
        src = pl.ds(pl.multiple_of(k * MAIN, MAIN), MAIN)
        dst = pl.ds(pl.multiple_of(i * MAIN, MAIN), MAIN)
        return (
            remote(red_m.at[g, src], back_m.at[dst], o_s.at[i, 0], o_r.at[i, 0], dev),
            remote(red_f.at[g, src], back_f.at[dst], o_s.at[i, 1], o_r.at[i, 1], dev),
        )

    def start(make, g):
        for d in range(2):
            for cp in make(g, d):
                cp.start()

    def arrived(make, g):
        for d in range(2):
            for cp in make(g, d):
                cp.wait_recv()

    def dispatch_group(g):
        @pl.loop(max(1, g * 8), g * 8 + 8)
        def _(i):
            for cp in inplane(i):
                cp.wait_recv()

        start(forward, g)

    def relay_group(g):
        arrived(forward, g)
        start(relay, g)

    perm_row = lax.broadcasted_iota(jnp.int32, (256, 256), 0)
    perm_col = lax.broadcasted_iota(jnp.int32, (256, 256), 1)

    def experts(g):
        arrived(relay, g)
        unfold = onehot(perm_col == (perm_row & 63) * 4 + (perm_row >> 6)).astype(BF)
        tail = jnp.dot(unfold, recv_f[g], preferred_element_type=F32).astype(BF)
        for k in range(4):
            recv_m[g, 256:320, k * QUART : (k + 1) * QUART] = tail[k * 64 : (k + 1) * 64, :]

        def hidden(cols):
            gate = jnp.dot(recv_m[g], wg[:, cols], preferred_element_type=F32)
            upv = jnp.dot(recv_m[g], wu[:, cols], preferred_element_type=F32)
            hid[:, cols] = (gate / (1.0 + jnp.exp(-gate)) * upv).astype(BF)

        @pl.loop(0, 5)
        def _(j):
            hidden(pl.ds(pl.multiple_of(j * 256, 256), 256))

        hidden(pl.ds(1280, 128))

        @pl.loop(0, 8)
        def _(j):
            cols = pl.ds(pl.multiple_of(j * 256, 256), 256)
            part_m[g, :, cols] = jnp.dot(
                hid[...], wd[:, cols], preferred_element_type=F32
            ).astype(BF)

        fold_back = onehot(perm_row == (perm_col & 63) * 4 + (perm_col >> 6)).astype(BF)
        stacked = jnp.concatenate(
            [part_m[g, 256:320, k * QUART : (k + 1) * QUART] for k in range(4)], axis=0
        )
        part_f[g] = jnp.dot(fold_back, stacked, preferred_element_type=F32).astype(BF)
        start(far, g)
        start(direct, g)

    def pass_sums(g):
        arrived(far, g)
        for d in range(2):
            own = pl.ds(64 if d == 0 else 224, 32)
            sum_m[g, d] = (part_m[g, own, :].astype(F32) + far_m[g, d].astype(F32)).astype(BF)
            sum_f[g, d] = (part_f[g, own, :].astype(F32) + far_f[g, d].astype(F32)).astype(BF)
        start(summed, g)

    def go_home(g):
        arrived(direct, g)
        arrived(summed, g)
        red_m[g] = (
            part_m[g, 0:64, :].astype(F32) + near_m[g, 0].astype(F32) + near_m[g, 1].astype(F32)
        ).astype(BF)
        red_f[g] = (
            part_f[g, 0:64, :].astype(F32) + near_f[g, 0].astype(F32) + near_f[g, 1].astype(F32)
        ).astype(BF)
        if g == 0:
            back_m[0:MAIN, :] = red_m[0, 0:MAIN, :]
            back_f[0:MAIN, :] = red_f[0, 0:MAIN, :]

        @pl.loop(1 if g == 0 else 0, 8)
        def _(k):
            for cp in home(g, k):
                cp.start()

    dispatch_group(0)
    dispatch_group(1)
    relay_group(0)
    dispatch_group(2)
    relay_group(1)
    dispatch_group(3)
    for ld in loads:
        ld.wait()
    experts(0)
    relay_group(2)
    experts(1)
    pass_sums(0)
    relay_group(3)
    experts(2)
    pass_sums(1)
    go_home(0)
    experts(3)
    pass_sums(2)
    go_home(1)
    pass_sums(3)
    go_home(2)
    go_home(3)

    cols_of = routes_cols(ids[...], y, x, c)
    lane = lax.broadcasted_iota(jnp.int32, (TOK, EXPERTS * MAIN), 1)

    @pl.loop(1, 32)
    def _(i):
        for cp in home(lax.div(i, 8), lax.rem(i, 8)):
            cp.wait_recv()

    for k in range(4):
        cols = slice(k * QUART, (k + 1) * QUART)
        total = mid[:, cols].astype(F32)
        for ch in range(TOP):
            main, tail = cols_of[ch]
            picked = jnp.dot(
                onehot(lane == main).astype(BF), back_m[:, cols], preferred_element_type=F32
            ) + jnp.dot(
                onehot(lane == tail * 4 + k).astype(BF), back_f[...], preferred_element_type=F32
            )
            total = total + picked * gates[:, ch : ch + 1]
        out[:, cols] = total.astype(BF)

    @pl.loop(1, 32)
    def _(i):
        for cp in inplane(i):
            cp.wait_send()
        for cp in home(lax.div(i, 8), lax.rem(i, 8)):
            cp.wait_send()

    for h in range(4):
        for r in (2, 1, 3):
            for p in range(3):
                send_head(h, r, p).wait_send()
            return_head(h, r).wait_send()
    swap_chip().wait_send()
    for i in range(1, 16):
        swap(i // 4, i % 4).wait_send()
    for d in range(2):
        ring(0, 0, d).wait_send()
        ring_relay(0, 0, d).wait_send()
        for a in range(4):
            ring(1, a, d).wait_send()
            ring_relay(1, a, d).wait_send()
    for g in range(GROUPS):
        for make in (forward, relay, far, direct, summed):
            for d in range(2):
                for cp in make(g, d):
                    cp.wait_send()


def layer(attn_inputs, residual, out_weight, gain, ids, gates, wg, wu, wd):
    vm = pl.BlockSpec(memory_space=pltpu.VMEM)
    hb = pl.BlockSpec(memory_space=pl.ANY)
    dma = pltpu.SemaphoreType.DMA
    G = GROUPS
    scratch = [
        pltpu.VMEM((3, 512, 512), BF),
        pltpu.VMEM((4, TOK, 512), BF),
        pltpu.VMEM((4, TOK, 512), BF),
        pltpu.VMEM((D, D), BF),
        pltpu.VMEM((TOK, D), BF),
        pltpu.VMEM((TOK, D), BF),
        pltpu.VMEM((D, FFL), BF),
        pltpu.VMEM((D, FFL), BF),
        pltpu.VMEM((FFL, D), BF),
        pltpu.VMEM((256, D), BF),
        pltpu.VMEM((256, QUART), BF),
        pltpu.VMEM((G, 320, D), BF),
        pltpu.VMEM((G, 256, QUART), BF),
        pltpu.VMEM((320, FFL), BF),
        pltpu.VMEM((G, 320, D), BF),
        pltpu.VMEM((G, 256, QUART), BF),
        pltpu.VMEM((G, 2, 32, D), BF),
        pltpu.VMEM((G, 2, 32, QUART), BF),
        pltpu.VMEM((G, 2, 32, D), BF),
        pltpu.VMEM((G, 2, 32, QUART), BF),
        pltpu.VMEM((G, 2, 64, D), BF),
        pltpu.VMEM((G, 2, 64, QUART), BF),
        pltpu.VMEM((G, 64, D), BF),
        pltpu.VMEM((G, 64, QUART), BF),
        pltpu.VMEM((256, D), BF),
        pltpu.VMEM((256, QUART), BF),
        dma((4,)),
        dma((4, 3, 3)),
        dma((4, 3, 3)),
        dma((4, 3)),
        dma((4, 3)),
        dma((5, 2, 2)),
        dma((5, 2, 2)),
        dma((16,)),
        dma((16,)),
        dma((3,)),
        dma((32, 2)),
        dma((32, 2)),
    ]
    scratch += [dma((G, 2, 2)) for _ in range(10)]
    scratch += [dma((32, 2)), dma((32, 2))]
    return pl.pallas_call(
        layer_kernel,
        out_shape=jax.ShapeDtypeStruct((TOK, D), BF),
        in_specs=[hb, vm, hb] + [vm] * 4 + [hb] * 3,
        out_specs=vm,
        scratch_shapes=scratch,
        name="layer",
        compiler_params=pltpu.CompilerParams(
            collective_id=0, has_side_effects=True, vmem_limit_bytes=60 * 2**20
        ),
    )(attn_inputs, residual, out_weight, gain, ids, ids.T, gates, wg, wu, wd)


def per_device(
    attn_inputs,
    residual,
    out_weight,
    norm_gain,
    expert_ids,
    gate_weights,
    gate_weight,
    up_weight,
    down_weight,
):
    result = layer(
        attn_inputs[0],
        residual[0],
        out_weight,
        norm_gain.reshape(1, D),
        expert_ids[0],
        gate_weights[0],
        gate_weight[0],
        up_weight[0],
        down_weight[0],
    )
    return result.reshape(1, TOK, D)


def solution(mesh):
    placed = (
        P("exp", "seq", None),
        P("exp", "seq", None),
        P("exp", None),
        P(),
        P("exp", "seq", None),
        P("exp", "seq", None),
        P("exp", None, "seq"),
        P("exp", None, "seq"),
        P("exp", "seq", None),
    )
    return jax.shard_map(
        per_device, mesh=mesh, in_specs=placed, out_specs=P("exp", "seq", None), check_vma=False
    )
```
